768 devices in a mesh: ctx: 96 (over z, x, core), fsdp: 8 (over y).
Axes of the slice: x: 4, y: 8, z: 12, core: 2. Of those that a mesh axis runs over, the one named last changes fastest.
Arguments:
- projected: bfloat16 [3, 24576, 8192], P(None, 'ctx', 'fsdp'), may hold values from -6 to 6
- short_weight: bfloat16 [3, 3, 8192], P(None, None, 'fsdp'), may hold values from -3 to 3
- rates: float32 [512, 16], P('fsdp'), may hold values from 1.2207031e-05 to 0.03
- residues: float32 [512, 16], P('fsdp'), may hold values from -0.12 to 0.12
- skip: float32 [8192], P('fsdp'), may hold values from -1 to 1
- residual: bfloat16 [24576, 8192], P('ctx', 'fsdp'), may hold values from -40 to 40
- gain: float32 [8192], P('fsdp'), may hold values from 0.5 to 1.5
Outputs:
- new_residual: bfloat16 [24576, 8192], P('ctx', 'fsdp')
- normed: bfloat16 [24576, 8192], P('ctx', 'fsdp')
The draws below stay inside these ranges and needn't reach their ends.
All inputs are finite; a program needn't handle non-finite values.
Results may differ from the reference program's by a relative error of at most 0.0047.
Values may be sent and summed in bfloat16 or wider, within the bound.
A program may use at most 64 MiB of HBM per device.

```python
import math
import jax
import jax.numpy as jnp
from jax import lax

D = 8192
CHANNELS_PER_GRP = 16
FILTER_MODES = 16
TAPS = 3
SEQ = 24576
GROUPS = 512


def draw_residual(key, part):
    columns = jnp.arange(D).astype(jnp.float32) / D
    column_scale = 10.0 ** (columns - 0.5)
    row_draw = jax.random.uniform(jax.random.fold_in(key, 1), (SEQ, 1), jnp.float32)
    row_scale = 10.0 ** (row_draw - 0.5)
    base = jnp.clip(jax.random.normal(jax.random.fold_in(key, 4), (SEQ, D), jnp.float32), -4.0, 4.0)
    return (base * row_scale * column_scale[None, :]).astype(jnp.bfloat16)


def shard_levels(stream_key, extent, shards, least, top_value):
    def one(dim, parts):
        heights = jax.random.uniform(jax.random.fold_in(jax.random.fold_in(stream_key, 6), dim), (parts,), jnp.float32, least / len(shards), top_value / len(shards))
        return jnp.repeat(jnp.exp(heights), extent[dim] // parts).reshape((-1,) + (1,) * (len(extent) - dim - 1))

    factor_of = one(*shards[0])
    for cut in shards[1:]:
        factor_of = factor_of * one(*cut)
    return factor_of


def scatter_about(key, dims, spread, most, cuts=(), dtype=jnp.bfloat16):
    array = jax.random.normal(key, dims, jnp.float32) * spread
    if len(cuts) > 0:
        array = shard_levels(key, dims, cuts, -0.22, 0.18) * array
    return jnp.clip(array, min=-most, max=most).astype(dtype)


def setup_inputs(seed: int = 0) -> dict:
    key_of = jax.random.split(jax.random.key(seed), 8)
    return {
        "projected": scatter_about(key_of[0], (3, SEQ, D), 1.0, 6.0, ((1, 96), (2, 8))),
        "short_weight": scatter_about(key_of[1], (TAPS, 3, D), 0.6, 3.0, ((2, 8),)),
        "rates": jnp.clip(jnp.exp(math.log(0.03) - 7.8069405 * jax.random.uniform(key_of[2], (GROUPS, FILTER_MODES), jnp.float32) ** shard_levels(key_of[2], (GROUPS, FILTER_MODES), ((0, 8),), -0.2, 0.2)), 1.220703143189894e-05, 0.03),
        "residues": scatter_about(key_of[3], (GROUPS, FILTER_MODES), 0.02, 0.12, ((0, 8),), jnp.float32),
        "skip": jnp.clip(jax.random.uniform(key_of[4], (D,), jnp.float32, -1.0, 1.0) * shard_levels(key_of[4], (D,), ((0, 8),), -0.4, 0.0), -1.0, 1.0),
        "residual": draw_residual(jax.random.fold_in(key_of[7], 71), 0),
        "gain": jnp.clip(1.0 + 0.1 * jax.random.normal(key_of[6], (D,), jnp.float32), 0.5, 1.5),
    }


def reference(projected, short_weight, rates, residues, skip, residual, gain):
    times_axis = jnp.arange(SEQ).astype(jnp.float32)
    filter_taps = jnp.zeros((GROUPS, SEQ), jnp.float32)
    for mode in range(FILTER_MODES):
        filter_taps = filter_taps + residues[:, mode:mode + 1] * jnp.exp(-rates[:, mode:mode + 1] * times_axis[None, :])
    column_block = min(D, 1024)
    pieces = []
    for block in range(D // column_block):
        lower = block * column_block
        upper = lower + column_block
        inputs = projected[:, :, lower:upper].astype(jnp.float32)
        weights = short_weight[:, :, lower:upper].astype(jnp.float32)
        padded_input = jnp.pad(inputs, ((0, 0), (TAPS - 1, 0), (0, 0)))
        filtered = jnp.zeros_like(inputs)
        for shift_amount in range(TAPS):
            lead = TAPS - 1 - shift_amount
            filtered = filtered + weights[shift_amount][:, None, :] * padded_input[:, lead:lead + SEQ, :]
        query_part = filtered[0]
        product = (filtered[1] * filtered[2]).astype(jnp.bfloat16)
        product_wide = product.astype(jnp.float32)
        channel_taps = jnp.repeat(filter_taps[lower // CHANNELS_PER_GRP:upper // CHANNELS_PER_GRP], CHANNELS_PER_GRP, axis=0).T
        spectrum = jnp.fft.rfft(product_wide, n=2 * SEQ, axis=0) * jnp.fft.rfft(channel_taps, n=2 * SEQ, axis=0)
        conv = jnp.fft.irfft(spectrum, n=2 * SEQ, axis=0)[:SEQ]
        summed_block = residual[:, lower:upper].astype(jnp.float32) + query_part * (conv + skip[None, lower:upper] * product_wide)
        pieces.append(summed_block)
    summed = jnp.concatenate(pieces, axis=1)
    new_residual = summed.astype(jnp.bfloat16)
    squares = lax.optimization_barrier(jnp.sum(summed * summed, axis=1, keepdims=True))
    normed = (summed * lax.rsqrt(squares / D + 1e-05) * gain[None, :]).astype(jnp.bfloat16)
    return (new_residual, normed)
```

```python
import functools

import jax
import jax.numpy as jnp
from jax import lax
from jax.experimental import pallas as pl
from jax.experimental.pallas import tpu as pltpu
from jax.sharding import PartitionSpec as P

CH = 16
MODES = 16
LANES = 128
GPB = LANES // CH
KB = GPB * MODES
ROW = 8
F32 = jnp.float32
BF16 = jnp.bfloat16
MESH = pl.DeviceIdType.MESH
REACH = 3
LOCAL_A = 4
LOCAL_B = 5


def iota(shape, dim):
    return lax.broadcasted_iota(jnp.int32, shape, dim)


def split(value):
    high = value.astype(BF16)
    return high, (value - high.astype(F32)).astype(BF16)


def mode_column(ref, block):
    groups = ref.shape[1]
    spread = jnp.broadcast_to(ref[...][None], (GPB, MODES, groups)).reshape(KB, groups)
    own = iota((KB, groups), 1) == block * GPB + iota((KB, groups), 0) // MODES
    return jnp.sum(jnp.where(own, spread, 0.0), axis=1, keepdims=True)


def as_row(column):
    same = iota((KB, KB), 0) == iota((KB, KB), 1)
    return jnp.sum(jnp.where(same, jnp.broadcast_to(column, (KB, KB)), 0.0), axis=0, keepdims=True)


def group_mask():
    return iota((KB, LANES), 0) // MODES == iota((KB, LANES), 1) // CH


def by_channel(column):
    spread = jnp.where(group_mask(), jnp.broadcast_to(column, (KB, LANES)), 0.0)
    return jnp.sum(spread.reshape(GPB, MODES, LANES), axis=0)


def short_conv(x, before, taps):
    sub = iota((8, x.shape[1]), 0)
    older, newer = before[0:1, :], before[1:2, :]
    one = pltpu.roll(x, 1, 0)
    two = pltpu.roll(x, 2, 0)
    one_top = jnp.where(sub == 0, newer, one[:8])
    two_top = jnp.where(sub == 0, older, jnp.where(sub == 1, newer, two[:8]))
    one = jnp.concatenate([one_top, one[8:]], axis=0)
    two = jnp.concatenate([two_top, two[8:]], axis=0)
    return taps[0] * x + taps[1] * one + taps[2] * two


def main_kernel(
    nz,
    ny,
    tokens,
    blocks,
    proj_hbm,
    resid_hbm,
    weight_hbm,
    rates_hbm,
    residues_hbm,
    skip_hbm,
    summed_ref,
    inv_ref,
    weight_ref,
    rates_ref,
    residues_ref,
    skip_ref,
    proj,
    resid,
    halo_out,
    halo_in,
    weights,
    p_buf,
    q_buf,
    base_buf,
    e_buf,
    f_buf,
    h_buf,
    edge_buf,
    s_buf,
    rs_buf,
    b_buf,
    c_buf,
    z_buf,
    x_out,
    x_buf,
    sq_acc,
    sq_out,
    sq_buf,
    load_sem,
    halo_sem,
    rs_send,
    rs_recv,
    z_send,
    z_recv,
    x_send,
    x_recv,
    y_send,
    y_recv,
):
    width = blocks * LANES
    ctx = lax.axis_index("ctx")
    y = lax.axis_index("fsdp")
    z = ctx // ROW
    me = ctx % ROW
    last = nz * ROW - 1
    loads = [
        pltpu.make_async_copy(proj_hbm.at[c], proj.at[c], load_sem.at[c]) for c in (1, 2, 0)
    ] + [pltpu.make_async_copy(resid_hbm, resid, load_sem.at[3])]
    small = [
        pltpu.make_async_copy(src, dst, load_sem.at[4 + k])
        for k, (src, dst) in enumerate(
            (
                (rates_hbm, rates_ref),
                (residues_hbm, residues_ref),
                (weight_hbm, weight_ref),
                (skip_hbm, skip_ref),
            )
        )
    ]
    for load in small + loads:
        load.start()
    barrier = pltpu.get_barrier_semaphore()

    def hello(**where):
        pl.semaphore_signal(barrier, inc=1, device_id=where, device_id_type=MESH)

    for k in range(1, REACH + 1):

        @pl.when(z >= k)
        def _():
            hello(ctx=ctx - k * ROW)

    for k in range(1, ROW):
        hello(ctx=z * ROW + (me + k) % ROW)
    for k in range(1, ny):
        hello(fsdp=(y + k) % ny)

    @pl.when(ctx > 0)
    def _():
        hello(ctx=ctx - 1)

    for load in small:
        load.wait()
    weights[...] = weight_ref[...].astype(F32)
    lag = (tokens - 1 - iota((1, tokens), 1)).astype(F32)

    def fill_states(block, carry):
        rate = mode_column(rates_ref, block)
        residue = mode_column(residues_ref, block)
        decay = jnp.exp(-rate * lag)
        high, low = split(decay)
        e_buf[block, pl.ds(0, KB), :] = high
        e_buf[block, pl.ds(KB, KB), :] = low
        edge_buf[block, 0] = by_channel(decay[:, 0:1])
        edge_buf[block, 1] = by_channel(decay[:, 1:2])
        h_buf[block] = jnp.sum((residue * decay).reshape(GPB, MODES, tokens), axis=1)
        return carry

    lax.fori_loop(0, blocks, fill_states, 0)
    for load in loads[:2]:
        load.wait()

    def taps_of(c, cols):
        return [weights[tap, c : c + 1, cols] for tap in range(3)]

    def states(block, carry):
        cols = pl.ds(pl.multiple_of(block * LANES, LANES), LANES)
        none = jnp.zeros((2, LANES), F32)
        key = short_conv(proj[1, :, cols].astype(F32), none, taps_of(1, cols))
        product = key * short_conv(proj[2, :, cols].astype(F32), none, taps_of(2, cols))
        top = jnp.where(iota((8, LANES), 0) < 2, 0.0, product[:8])
        product = jnp.concatenate([top, product[8:]], axis=0).astype(BF16)
        p_buf[block] = product
        both = jnp.dot(e_buf[block], product, preferred_element_type=F32)
        total = jnp.where(group_mask(), both[:KB] + both[KB:], 0.0)
        s_buf[block] = jnp.sum(total.reshape(GPB, MODES, LANES), axis=0)
        return carry

    lax.fori_loop(0, blocks, states, 0)
    loads[2].wait()
    for c in range(3):
        halo_out[c] = proj[c, tokens - 16 :, :].astype(F32)[14:16]

    reach = jnp.minimum(nz - 1 - z, REACH)
    pl.semaphore_wait(barrier, ROW - 1 + ny - 1 + reach + jnp.minimum(last - ctx, 1))

    def halo_copy():
        return pltpu.make_async_remote_copy(
            src_ref=halo_out,
            dst_ref=halo_in,
            send_sem=halo_sem.at[0],
            recv_sem=halo_sem.at[1],
            device_id={"ctx": jnp.minimum(ctx + 1, last)},
            device_id_type=MESH,
        )

    @pl.when(ctx < last)
    def _():
        halo_copy().start()

    @pl.when(ctx == 0)
    def _():
        halo_in[...] = jnp.zeros_like(halo_in)

    @pl.when(ctx > 0)
    def _():
        halo_copy().wait_recv()

    def filtered(c, cols):
        return short_conv(proj[c, :, cols].astype(F32), halo_in[c, :, cols], taps_of(c, cols))

    def first_rows(c):
        every = slice(None)
        return short_conv(proj[c, :16, :].astype(F32), halo_in[c], taps_of(c, every))

    product_top = (first_rows(1) * first_rows(2)).astype(BF16)
    for block in range(blocks):
        top = product_top[:, block * LANES : (block + 1) * LANES]
        p_buf[block, pl.ds(0, 16), :] = top
        wide_top = top.astype(F32)
        s_buf[block] += edge_buf[block, 0] * wide_top[0:1] + edge_buf[block, 1] * wide_top[1:2]

    def rs_copy(k, slot, target):
        return pltpu.make_async_remote_copy(
            src_ref=s_buf.at[target],
            dst_ref=rs_buf.at[slot],
            send_sem=rs_send.at[k],
            recv_sem=rs_recv.at[slot],
            device_id={"ctx": z * ROW + target},
            device_id_type=MESH,
        )

    for k in range(1, ROW):
        rs_copy(k, me, (me + k) % ROW).start()
    rs_buf[me] = s_buf[me]

    loads[3].wait()
    lag_next = (iota((tokens, 1), 0) + 1).astype(F32)

    def local(block, carry):
        cols = pl.ds(pl.multiple_of(block * LANES, LANES), LANES)
        rate = as_row(mode_column(rates_ref, block))
        residue = as_row(mode_column(residues_ref, block))
        high, low = split(residue * jnp.exp(-rate * lag_next))
        f_buf[block, :, pl.ds(0, KB)] = high
        f_buf[block, :, pl.ds(KB, KB)] = low
        product = p_buf[block]
        half = tokens // 2
        lane_group = iota((tokens, LANES), 1) // CH
        causal = iota((half, half), 1) <= iota((half, half), 0)
        taps = h_buf[block]
        total = jnp.zeros((tokens, LANES), F32)
        for g in range(GPB):
            row = jnp.broadcast_to(taps[g : g + 1], (half, tokens))
            rolled = pltpu.roll(row, half + 1, 1, stride=1, stride_axis=0)
            far = rolled[:, :half].astype(BF16)
            near = jnp.where(causal, rolled[:, half:], 0.0).astype(BF16)
            matrix = jnp.concatenate(
                [
                    jnp.concatenate([near, jnp.zeros_like(near)], axis=1),
                    jnp.concatenate([far, near], axis=1),
                ],
                axis=0,
            )
            part = jnp.where(lane_group == g, product, jnp.zeros_like(product))
            total = total + jnp.dot(matrix, part, preferred_element_type=F32)
        query = filtered(0, cols)
        q_buf[block] = query
        wide = product.astype(F32)
        base_buf[block] = resid[:, cols].astype(F32) + query * (total + skip_ref[:, cols] * wide)
        return carry

    lax.fori_loop(0, LOCAL_A, local, 0)

    rate = by_channel(mode_column(rates_ref, me))
    one_block = jnp.exp(-rate * float(tokens))
    one_row = jnp.exp(-rate * float(tokens * ROW))
    for k in range(1, ROW):
        source = (me + ROW - k) % ROW
        rs_copy(k, source, me).wait_recv()
    prefixes = [jnp.zeros((MODES, LANES), F32)]
    for i in range(ROW):
        prefixes.append(one_block * prefixes[-1] + rs_buf[i])
    b_buf[0] = prefixes[ROW]

    def z_copy(k):
        return pltpu.make_async_remote_copy(
            src_ref=b_buf.at[k // REACH],
            dst_ref=z_buf.at[k],
            send_sem=z_send.at[k],
            recv_sem=z_recv.at[k],
            device_id={"ctx": jnp.minimum(ctx + k * ROW, last)},
            device_id_type=MESH,
        )

    for k in range(1, REACH):

        @pl.when(z + k < nz)
        def _():
            z_copy(k).start()

    lax.fori_loop(LOCAL_A, LOCAL_B, local, 0)

    c_buf[...] = jnp.zeros_like(c_buf)
    for k in range(REACH, 0, -1):

        @pl.when(k <= z)
        def _():
            z_copy(k).wait_recv()
            c_buf[...] = one_row * c_buf[...] + z_buf[k]

    entering = c_buf[...]
    b_buf[1] = one_row * entering + prefixes[ROW]

    @pl.when(z + REACH < nz)
    def _():
        z_copy(REACH).start()

    for i in range(ROW):
        value = jnp.exp(-rate * float(tokens * i)) * entering + prefixes[i]
        x_out[i] = value.astype(x_out.dtype)

    def x_copy(k, slot, target):
        return pltpu.make_async_remote_copy(
            src_ref=x_out.at[target],
            dst_ref=x_buf.at[slot],
            send_sem=x_send.at[k],
            recv_sem=x_recv.at[slot],
            device_id={"ctx": z * ROW + target},
            device_id_type=MESH,
        )

    for k in range(1, ROW):
        x_copy(k, me, (me + k) % ROW).start()
    x_buf[me] = x_out[me]
    lax.fori_loop(LOCAL_B, blocks, local, 0)
    sq_acc[...] = jnp.zeros_like(sq_acc)
    for k in range(1, ROW):
        x_copy(k, (me + ROW - k) % ROW, me).wait_recv()

    def finish(block, carry):
        cols = pl.ds(pl.multiple_of(block * LANES, LANES), LANES)
        state = jnp.broadcast_to(x_buf[block].astype(F32)[None], (GPB, MODES, LANES)).reshape(KB, LANES)
        state = jnp.where(group_mask(), state, 0.0).astype(BF16)
        carried = jnp.dot(
            f_buf[block], jnp.concatenate([state, state], axis=0), preferred_element_type=F32
        )
        summed = base_buf[block] + q_buf[block] * carried
        summed_ref[:, cols] = summed
        sq_acc[...] += summed * summed
        return carry

    lax.fori_loop(0, blocks, finish, 0)
    ones = jnp.ones((8, LANES), BF16)
    contract = (((1,), (1,)), ((), ()))
    high, low = split(sq_acc[...])
    squares = lax.dot_general(ones, high, contract, preferred_element_type=F32) + lax.dot_general(
        ones, low, contract, preferred_element_type=F32
    )
    sq_out[...] = squares[:1]

    def y_copy(k, slot, target):
        return pltpu.make_async_remote_copy(
            src_ref=sq_out,
            dst_ref=sq_buf.at[slot],
            send_sem=y_send.at[k],
            recv_sem=y_recv.at[slot],
            device_id={"fsdp": target},
            device_id_type=MESH,
        )

    for k in range(1, ny):
        y_copy(k, y, (y + k) % ny).start()
    sq_buf[y] = sq_out[...]
    for k in range(1, ny):
        y_copy(k, (y + ny - k) % ny, y).wait_recv()
    total = sq_buf[0]
    for k in range(1, ny):
        total = total + sq_buf[k]
    scale = lax.rsqrt(total / float(width * ny) + 1e-05)
    inv_ref[...] = jnp.transpose(jnp.broadcast_to(scale, (LANES, tokens)))

    @pl.when(ctx < last)
    def _():
        halo_copy().wait_send()

    for k in range(1, ROW):
        rs_copy(k, me, (me + k) % ROW).wait_send()
        x_copy(k, me, (me + k) % ROW).wait_send()
    for k in range(1, REACH + 1):

        @pl.when(z + k < nz)
        def _():
            z_copy(k).wait_send()

    for k in range(1, ny):
        y_copy(k, y, (y + k) % ny).wait_send()


def per_device(nz, ny, projected, short_weight, rates, residues, skip, residual, gain):
    tokens, width = residual.shape
    blocks = width // LANES
    vmem = pl.BlockSpec(memory_space=pltpu.VMEM)
    hbm = pl.BlockSpec(memory_space=pltpu.HBM)
    dma = pltpu.SemaphoreType.DMA
    summed, inv = pl.pallas_call(
        functools.partial(main_kernel, nz, ny, tokens, blocks),
        out_shape=(
            jax.ShapeDtypeStruct((tokens, width), F32),
            jax.ShapeDtypeStruct((tokens, LANES), F32),
        ),
        in_specs=[hbm] * 6,
        out_specs=(vmem, vmem),
        scratch_shapes=[
            pltpu.VMEM(short_weight.shape, BF16),
            pltpu.VMEM((MODES, width // CH), F32),
            pltpu.VMEM((MODES, width // CH), F32),
            pltpu.VMEM((1, width), F32),
            pltpu.VMEM((3, tokens, width), BF16),
            pltpu.VMEM((tokens, width), BF16),
            pltpu.VMEM((3, 2, width), F32),
            pltpu.VMEM((3, 2, width), F32),
            pltpu.VMEM((3, 3, width), F32),
            pltpu.VMEM((blocks, tokens, LANES), BF16),
            pltpu.VMEM((blocks, tokens, LANES), F32),
            pltpu.VMEM((blocks, tokens, LANES), F32),
            pltpu.VMEM((blocks, 2 * KB, tokens), BF16),
            pltpu.VMEM((blocks, tokens, 2 * KB), BF16),
            pltpu.VMEM((blocks, GPB, tokens), F32),
            pltpu.VMEM((blocks, 2, MODES, LANES), F32),
            pltpu.VMEM((ROW, MODES, LANES), F32),
            pltpu.VMEM((ROW, MODES, LANES), F32),
            pltpu.VMEM((2, MODES, LANES), F32),
            pltpu.VMEM((MODES, LANES), F32),
            pltpu.VMEM((REACH + 1, MODES, LANES), F32),
            pltpu.VMEM((ROW, MODES, LANES), BF16),
            pltpu.VMEM((ROW, MODES, LANES), BF16),
            pltpu.VMEM((tokens, LANES), F32),
            pltpu.VMEM((1, tokens), F32),
            pltpu.VMEM((ny, 1, tokens), F32),
            dma((8,)),
            dma((2,)),
            dma((ROW,)),
            dma((ROW,)),
            dma((REACH + 1,)),
            dma((REACH + 1,)),
            dma((ROW,)),
            dma((ROW,)),
            dma((ny,)),
            dma((ny,)),
        ],
        compiler_params=pltpu.CompilerParams(
            collective_id=0, has_side_effects=True, vmem_limit_bytes=40 << 20
        ),
        name="scan_conv",
    )(
        *[
            pltpu.with_memory_space_constraint(operand, pltpu.HBM)
            for operand in (
                projected,
                residual,
                short_weight,
                rates.T,
                residues.T,
                skip.reshape(1, width),
            )
        ]
    )
    new_residual = summed.astype(BF16)
    normed = (summed * inv[:, :1] * gain[None, :]).astype(BF16)
    return new_residual, normed


def solution(mesh):
    nz = mesh.shape["ctx"] // ROW
    ny = mesh.shape["fsdp"]
    return jax.shard_map(
        functools.partial(per_device, nz, ny),
        mesh=mesh,
        in_specs=(
            P(None, "ctx", "fsdp"),
            P(None, None, "fsdp"),
            P("fsdp", None),
            P("fsdp", None),
            P("fsdp"),
            P("ctx", "fsdp"),
            P("fsdp"),
        ),
        out_specs=(P("ctx", "fsdp"), P("ctx", "fsdp")),
        check_vma=False,
    )
```

```python
import functools

import jax
import jax.numpy as jnp
from jax import lax
from jax.experimental import pallas as pl
from jax.experimental.pallas import tpu as pltpu
from jax.sharding import PartitionSpec as P

CH = 16
MODES = 16
LANES = 128
GPB = LANES // CH
KB = GPB * MODES
ROW = 8
F32 = jnp.float32
BF16 = jnp.bfloat16
MESH = pl.DeviceIdType.MESH
REACH = 3
LOCAL_A = 1
LOCAL_B = 4
SENT = MODES + 8


def iota(shape, dim):
    return lax.broadcasted_iota(jnp.int32, shape, dim)


def split(value):
    high = value.astype(BF16)
    return high, (value - high.astype(F32)).astype(BF16)


def mode_column(ref, block):
    groups = ref.shape[1]
    spread = jnp.broadcast_to(ref[...][None], (GPB, MODES, groups)).reshape(KB, groups)
    own = iota((KB, groups), 1) == block * GPB + iota((KB, groups), 0) // MODES
    return jnp.sum(jnp.where(own, spread, 0.0), axis=1, keepdims=True)


def as_row(column):
    same = iota((KB, KB), 0) == iota((KB, KB), 1)
    return jnp.sum(jnp.where(same, jnp.broadcast_to(column, (KB, KB)), 0.0), axis=0, keepdims=True)


def group_mask():
    return iota((KB, LANES), 0) // MODES == iota((KB, LANES), 1) // CH


def by_channel(column):
    spread = jnp.where(group_mask(), jnp.broadcast_to(column, (KB, LANES)), 0.0)
    return jnp.sum(spread.reshape(GPB, MODES, LANES), axis=0)


def short_conv(x, before, taps):
    sub = iota((8, x.shape[1]), 0)
    older, newer = before[0:1, :], before[1:2, :]
    one = pltpu.roll(x, 1, 0)
    two = pltpu.roll(x, 2, 0)
    one_top = jnp.where(sub == 0, newer, one[:8])
    two_top = jnp.where(sub == 0, older, jnp.where(sub == 1, newer, two[:8]))
    one = jnp.concatenate([one_top, one[8:]], axis=0)
    two = jnp.concatenate([two_top, two[8:]], axis=0)
    return taps[0] * x + taps[1] * one + taps[2] * two


def main_kernel(
    nz,
    ny,
    tokens,
    blocks,
    proj_hbm,
    resid_hbm,
    weight_hbm,
    rates_hbm,
    residues_hbm,
    skip_hbm,
    summed_ref,
    inv_ref,
    weight_ref,
    rates_ref,
    residues_ref,
    skip_ref,
    proj,
    resid,
    halo_out,
    halo_in,
    weights,
    p_buf,
    q_buf,
    base_buf,
    e_buf,
    f_buf,
    h_buf,
    edge_buf,
    edge_in,
    s_buf,
    rs_buf,
    b_buf,
    c_buf,
    z_buf,
    x_out,
    x_buf,
    sq_acc,
    sq_out,
    sq_buf,
    load_sem,
    halo_sem,
    edge_send,
    edge_recv,
    rs_send,
    rs_recv,
    z_send,
    z_recv,
    x_send,
    x_recv,
    y_send,
    y_recv,
):
    width = blocks * LANES
    ctx = lax.axis_index("ctx")
    y = lax.axis_index("fsdp")
    z = ctx // ROW
    me = ctx % ROW
    last = nz * ROW - 1
    loads = [
        pltpu.make_async_copy(proj_hbm.at[c], proj.at[c], load_sem.at[c]) for c in (1, 2, 0)
    ] + [pltpu.make_async_copy(resid_hbm, resid, load_sem.at[3])]
    small = [
        pltpu.make_async_copy(src, dst, load_sem.at[4 + k])
        for k, (src, dst) in enumerate(
            (
                (rates_hbm, rates_ref),
                (residues_hbm, residues_ref),
                (weight_hbm, weight_ref),
                (skip_hbm, skip_ref),
            )
        )
    ]
    for load in small + loads:
        load.start()
    barrier = pltpu.get_barrier_semaphore()

    def hello(**where):
        pl.semaphore_signal(barrier, inc=1, device_id=where, device_id_type=MESH)

    for k in range(1, REACH + 1):

        @pl.when(z >= k)
        def _():
            hello(ctx=ctx - k * ROW)

    for k in range(1, ROW):
        hello(ctx=z * ROW + (me + k) % ROW)
    for k in range(1, ny):
        hello(fsdp=(y + k) % ny)

    @pl.when((z > 0) & (me < ROW - 1))
    def _():
        hello(ctx=z * ROW - 1)

    for load in small:
        load.wait()
    weights[...] = weight_ref[...].astype(F32)
    lag = (tokens - 1 - iota((1, tokens), 1)).astype(F32)

    def fill_states(block, carry):
        rate = mode_column(rates_ref, block)
        residue = mode_column(residues_ref, block)
        decay = jnp.exp(-rate * lag)
        high, low = split(decay)
        e_buf[block, pl.ds(0, KB), :] = high
        e_buf[block, pl.ds(KB, KB), :] = low
        edge_buf[block, 0] = by_channel(decay[:, 0:1])
        edge_buf[block, 1] = by_channel(decay[:, 1:2])
        h_buf[block] = jnp.sum((residue * decay).reshape(GPB, MODES, tokens), axis=1)
        return carry

    lax.fori_loop(0, blocks, fill_states, 0)
    for load in loads[:2]:
        load.wait()

    def taps_of(c, cols):
        return [weights[tap, c : c + 1, cols] for tap in range(3)]

    def states(block, carry):
        cols = pl.ds(pl.multiple_of(block * LANES, LANES), LANES)
        none = jnp.zeros((2, LANES), F32)
        key = short_conv(proj[1, :, cols].astype(F32), none, taps_of(1, cols))
        product = key * short_conv(proj[2, :, cols].astype(F32), none, taps_of(2, cols))
        top = jnp.where(iota((8, LANES), 0) < 2, 0.0, product[:8])
        product = jnp.concatenate([top, product[8:]], axis=0).astype(BF16)
        p_buf[block] = product
        both = jnp.dot(e_buf[block], product, preferred_element_type=F32)
        total = jnp.where(group_mask(), both[:KB] + both[KB:], 0.0)
        s_buf[block, pl.ds(0, MODES), :] = jnp.sum(total.reshape(GPB, MODES, LANES), axis=0)
        return carry

    for c in (1, 2):
        tail = proj[c, tokens - 16 :, :].astype(F32)[14:16]
        head = proj[c, :16, :].astype(F32)[:2]
        halo_out[c] = tail
        for block in range(blocks):
            mine = slice(block * LANES, (block + 1) * LANES)
            s_buf[block, pl.ds(MODES + 2 * c - 2, 2), :] = tail[:, mine]
            s_buf[block, pl.ds(MODES + 2 * c + 2, 2), :] = head[:, mine]
    lax.fori_loop(0, blocks, states, 0)
    loads[2].wait()
    halo_out[0] = proj[0, tokens - 16 :, :].astype(F32)[14:16]

    reach = jnp.minimum(nz - 1 - z, REACH)
    fan = jnp.minimum(reach, 1) * (me // (ROW - 1)) * (ROW - 1)
    pl.semaphore_wait(barrier, ROW - 1 + ny - 1 + reach + fan)

    def rs_copy(k, slot, target):
        return pltpu.make_async_remote_copy(
            src_ref=s_buf.at[target],
            dst_ref=rs_buf.at[slot],
            send_sem=rs_send.at[k],
            recv_sem=rs_recv.at[slot],
            device_id={"ctx": z * ROW + target},
            device_id_type=MESH,
        )

    def edge_copy(k):
        return pltpu.make_async_remote_copy(
            src_ref=s_buf.at[k, pl.ds(MODES, 8)],
            dst_ref=edge_in,
            send_sem=edge_send.at[k],
            recv_sem=edge_recv,
            device_id={"ctx": jnp.minimum(z * ROW + ROW + k, last)},
            device_id_type=MESH,
        )

    feeds = (me == ROW - 1) & (z < nz - 1)

    @pl.when(feeds)
    def _():
        for k in range(ROW):
            edge_copy(k).start()

    for k in range(1, ROW):
        rs_copy(k, me, (me + k) % ROW).start()
    rs_buf[me] = s_buf[me]

    def halo_copy():
        return pltpu.make_async_remote_copy(
            src_ref=halo_out,
            dst_ref=halo_in,
            send_sem=halo_sem.at[0],
            recv_sem=halo_sem.at[1],
            device_id={"ctx": jnp.minimum(ctx + 1, last)},
            device_id_type=MESH,
        )

    @pl.when(ctx < last)
    def _():
        halo_copy().start()

    @pl.when(ctx == 0)
    def _():
        halo_in[...] = jnp.zeros_like(halo_in)

    @pl.when(ctx > 0)
    def _():
        halo_copy().wait_recv()

    def filtered(c, cols):
        return short_conv(proj[c, :, cols].astype(F32), halo_in[c, :, cols], taps_of(c, cols))

    def first_rows(c):
        every = slice(None)
        return short_conv(proj[c, :16, :].astype(F32), halo_in[c], taps_of(c, every))

    product_top = (first_rows(1) * first_rows(2)).astype(BF16)
    for block in range(blocks):
        p_buf[block, pl.ds(0, 16), :] = product_top[:, block * LANES : (block + 1) * LANES]

    loads[3].wait()
    lag_next = (iota((tokens, 1), 0) + 1).astype(F32)

    def local(block, carry):
        cols = pl.ds(pl.multiple_of(block * LANES, LANES), LANES)
        rate = as_row(mode_column(rates_ref, block))
        residue = as_row(mode_column(residues_ref, block))
        high, low = split(residue * jnp.exp(-rate * lag_next))
        f_buf[block, :, pl.ds(0, KB)] = high
        f_buf[block, :, pl.ds(KB, KB)] = low
        product = p_buf[block]
        half = tokens // 2
        lane_group = iota((tokens, LANES), 1) // CH
        causal = iota((half, half), 1) <= iota((half, half), 0)
        taps = h_buf[block]
        total = jnp.zeros((tokens, LANES), F32)
        for g in range(GPB):
            row = jnp.broadcast_to(taps[g : g + 1], (half, tokens))
            rolled = pltpu.roll(row, half + 1, 1, stride=1, stride_axis=0)
            far = rolled[:, :half].astype(BF16)
            near = jnp.where(causal, rolled[:, half:], 0.0).astype(BF16)
            matrix = jnp.concatenate(
                [
                    jnp.concatenate([near, jnp.zeros_like(near)], axis=1),
                    jnp.concatenate([far, near], axis=1),
                ],
                axis=0,
            )
            part = jnp.where(lane_group == g, product, jnp.zeros_like(product))
            total = total + jnp.dot(matrix, part, preferred_element_type=F32)
        query = filtered(0, cols)
        q_buf[block] = query
        wide = product.astype(F32)
        base_buf[block] = resid[:, cols].astype(F32) + query * (total + skip_ref[:, cols] * wide)
        return carry

    lax.fori_loop(0, LOCAL_A, local, 0)

    rate = by_channel(mode_column(rates_ref, me))
    one_block = jnp.exp(-rate * float(tokens))
    one_row = jnp.exp(-rate * float(tokens * ROW))
    for k in range(1, ROW):
        source = (me + ROW - k) % ROW
        rs_copy(k, source, me).wait_recv()

    @pl.when(z == 0)
    def _():
        edge_in[...] = jnp.zeros_like(edge_in)

    @pl.when(z > 0)
    def _():
        edge_copy(0).wait_recv()

    mine = pl.ds(pl.multiple_of(me * LANES, LANES), LANES)
    key_taps, value_taps = taps_of(1, mine), taps_of(2, mine)

    def first_two(before, at, taps):
        now = rs_buf[at, pl.ds(MODES + 4, 4), :]
        out = []
        for c, w in enumerate(taps):
            older = before[2 * c : 2 * c + 1]
            newer = before[2 * c + 1 : 2 * c + 2]
            first = now[2 * c : 2 * c + 1]
            second = now[2 * c + 1 : 2 * c + 2]
            out.append(
                (
                    w[0] * first + w[1] * newer + w[2] * older,
                    w[0] * second + w[1] * first + w[2] * newer,
                )
            )
        return [(out[0][i] * out[1][i]).astype(BF16).astype(F32) for i in range(2)]

    prefixes = [jnp.zeros((MODES, LANES), F32)]
    for i in range(ROW):
        before = edge_in[:4, :] if i == 0 else rs_buf[i - 1, pl.ds(MODES, 4), :]
        one, two = first_two(before, i, (key_taps, value_taps))
        state = rs_buf[i, pl.ds(0, MODES), :] + edge_buf[me, 0] * one + edge_buf[me, 1] * two
        prefixes.append(one_block * prefixes[-1] + state)
    b_buf[0] = prefixes[ROW]

    def z_copy(k):
        return pltpu.make_async_remote_copy(
            src_ref=b_buf.at[k // REACH],
            dst_ref=z_buf.at[k],
            send_sem=z_send.at[k],
            recv_sem=z_recv.at[k],
            device_id={"ctx": jnp.minimum(ctx + k * ROW, last)},
            device_id_type=MESH,
        )

    for k in range(1, REACH):

        @pl.when(z + k < nz)
        def _():
            z_copy(k).start()

    lax.fori_loop(LOCAL_A, LOCAL_B, local, 0)

    c_buf[...] = jnp.zeros_like(c_buf)
    for k in range(REACH, 0, -1):

        @pl.when(k <= z)
        def _():
            z_copy(k).wait_recv()
            c_buf[...] = one_row * c_buf[...] + z_buf[k]

    entering = c_buf[...]
    b_buf[1] = one_row * entering + prefixes[ROW]

    @pl.when(z + REACH < nz)
    def _():
        z_copy(REACH).start()

    for i in range(ROW):
        value = jnp.exp(-rate * float(tokens * i)) * entering + prefixes[i]
        x_out[i] = value.astype(x_out.dtype)

    def x_copy(k, slot, target):
        return pltpu.make_async_remote_copy(
            src_ref=x_out.at[target],
            dst_ref=x_buf.at[slot],
            send_sem=x_send.at[k],
            recv_sem=x_recv.at[slot],
            device_id={"ctx": z * ROW + target},
            device_id_type=MESH,
        )

    for k in range(1, ROW):
        x_copy(k, me, (me + k) % ROW).start()
    x_buf[me] = x_out[me]
    lax.fori_loop(LOCAL_B, blocks, local, 0)
    sq_acc[...] = jnp.zeros_like(sq_acc)
    for k in range(1, ROW):
        x_copy(k, (me + ROW - k) % ROW, me).wait_recv()

    def finish(block, carry):
        cols = pl.ds(pl.multiple_of(block * LANES, LANES), LANES)
        state = jnp.broadcast_to(x_buf[block].astype(F32)[None], (GPB, MODES, LANES)).reshape(KB, LANES)
        state = jnp.where(group_mask(), state, 0.0).astype(BF16)
        carried = jnp.dot(
            f_buf[block], jnp.concatenate([state, state], axis=0), preferred_element_type=F32
        )
        summed = base_buf[block] + q_buf[block] * carried
        summed_ref[:, cols] = summed
        sq_acc[...] += summed * summed
        return carry

    lax.fori_loop(0, blocks, finish, 0)
    ones = jnp.ones((8, LANES), BF16)
    contract = (((1,), (1,)), ((), ()))
    high, low = split(sq_acc[...])
    squares = lax.dot_general(ones, high, contract, preferred_element_type=F32) + lax.dot_general(
        ones, low, contract, preferred_element_type=F32
    )
    sq_out[...] = squares[:1]

    def y_copy(k, slot, target):
        return pltpu.make_async_remote_copy(
            src_ref=sq_out,
            dst_ref=sq_buf.at[slot],
            send_sem=y_send.at[k],
            recv_sem=y_recv.at[slot],
            device_id={"fsdp": target},
            device_id_type=MESH,
        )

    for k in range(1, ny):
        y_copy(k, y, (y + k) % ny).start()
    sq_buf[y] = sq_out[...]
    for k in range(1, ny):
        y_copy(k, (y + ny - k) % ny, y).wait_recv()
    total = sq_buf[0]
    for k in range(1, ny):
        total = total + sq_buf[k]
    scale = lax.rsqrt(total / float(width * ny) + 1e-05)
    inv_ref[...] = jnp.transpose(jnp.broadcast_to(scale, (LANES, tokens)))

    @pl.when(ctx < last)
    def _():
        halo_copy().wait_send()

    @pl.when(feeds)
    def _():
        for k in range(ROW):
            edge_copy(k).wait_send()

    for k in range(1, ROW):
        rs_copy(k, me, (me + k) % ROW).wait_send()
        x_copy(k, me, (me + k) % ROW).wait_send()
    for k in range(1, REACH + 1):

        @pl.when(z + k < nz)
        def _():
            z_copy(k).wait_send()

    for k in range(1, ny):
        y_copy(k, y, (y + k) % ny).wait_send()


def per_device(nz, ny, projected, short_weight, rates, residues, skip, residual, gain):
    tokens, width = residual.shape
    blocks = width // LANES
    vmem = pl.BlockSpec(memory_space=pltpu.VMEM)
    hbm = pl.BlockSpec(memory_space=pltpu.HBM)
    dma = pltpu.SemaphoreType.DMA
    summed, inv = pl.pallas_call(
        functools.partial(main_kernel, nz, ny, tokens, blocks),
        out_shape=(
            jax.ShapeDtypeStruct((tokens, width), F32),
            jax.ShapeDtypeStruct((tokens, LANES), F32),
        ),
        in_specs=[hbm] * 6,
        out_specs=(vmem, vmem),
        scratch_shapes=[
            pltpu.VMEM(short_weight.shape, BF16),
            pltpu.VMEM((MODES, width // CH), F32),
            pltpu.VMEM((MODES, width // CH), F32),
            pltpu.VMEM((1, width), F32),
            pltpu.VMEM((3, tokens, width), BF16),
            pltpu.VMEM((tokens, width), BF16),
            pltpu.VMEM((3, 2, width), F32),
            pltpu.VMEM((3, 2, width), F32),
            pltpu.VMEM((3, 3, width), F32),
            pltpu.VMEM((blocks, tokens, LANES), BF16),
            pltpu.VMEM((blocks, tokens, LANES), F32),
            pltpu.VMEM((blocks, tokens, LANES), F32),
            pltpu.VMEM((blocks, 2 * KB, tokens), BF16),
            pltpu.VMEM((blocks, tokens, 2 * KB), BF16),
            pltpu.VMEM((blocks, GPB, tokens), F32),
            pltpu.VMEM((blocks, 2, MODES, LANES), F32),
            pltpu.VMEM((8, LANES), F32),
            pltpu.VMEM((ROW, SENT, LANES), F32),
            pltpu.VMEM((ROW, SENT, LANES), F32),
            pltpu.VMEM((2, MODES, LANES), F32),
            pltpu.VMEM((MODES, LANES), F32),
            pltpu.VMEM((REACH + 1, MODES, LANES), F32),
            pltpu.VMEM((ROW, MODES, LANES), BF16),
            pltpu.VMEM((ROW, MODES, LANES), BF16),
            pltpu.VMEM((tokens, LANES), F32),
            pltpu.VMEM((1, tokens), F32),
            pltpu.VMEM((ny, 1, tokens), F32),
            dma((8,)),
            dma((2,)),
            dma((ROW,)),
            dma,
            dma((ROW,)),
            dma((ROW,)),
            dma((REACH + 1,)),
            dma((REACH + 1,)),
            dma((ROW,)),
            dma((ROW,)),
            dma((ny,)),
            dma((ny,)),
        ],
        compiler_params=pltpu.CompilerParams(
            collective_id=0, has_side_effects=True, vmem_limit_bytes=40 << 20
        ),
        name="scan_conv",
    )(
        *[
            pltpu.with_memory_space_constraint(operand, pltpu.HBM)
            for operand in (
                projected,
                residual,
                short_weight,
                rates.T,
                residues.T,
                skip.reshape(1, width),
            )
        ]
    )
    new_residual = summed.astype(BF16)
    normed = (summed * inv[:, :1] * gain[None, :]).astype(BF16)
    return new_residual, normed


def solution(mesh):
    nz = mesh.shape["ctx"] // ROW
    ny = mesh.shape["fsdp"]
    return jax.shard_map(
        functools.partial(per_device, nz, ny),
        mesh=mesh,
        in_specs=(
            P(None, "ctx", "fsdp"),
            P(None, None, "fsdp"),
            P("fsdp", None),
            P("fsdp", None),
            P("fsdp"),
            P("ctx", "fsdp"),
            P("fsdp"),
        ),
        out_specs=(P("ctx", "fsdp"), P("ctx", "fsdp")),
        check_vma=False,
    )
```

```python
import functools

import jax
import jax.numpy as jnp
from jax import lax
from jax.experimental import pallas as pl
from jax.experimental.pallas import tpu as pltpu
from jax.sharding import PartitionSpec as P

CH = 16
MODES = 16
LANES = 128
GPB = LANES // CH
KB = GPB * MODES
ROW = 8
F32 = jnp.float32
BF16 = jnp.bfloat16
MESH = pl.DeviceIdType.MESH
REACH = 3
NEAR = 7
LOCAL_A = 1
LOCAL_B = 4
SENT = MODES + 8


def iota(shape, dim):
    return lax.broadcasted_iota(jnp.int32, shape, dim)


def split(value):
    high = value.astype(BF16)
    return high, (value - high.astype(F32)).astype(BF16)


def mode_column(ref, block):
    groups = ref.shape[1]
    spread = jnp.broadcast_to(ref[...][None], (GPB, MODES, groups)).reshape(KB, groups)
    own = iota((KB, groups), 1) == block * GPB + iota((KB, groups), 0) // MODES
    return jnp.sum(jnp.where(own, spread, 0.0), axis=1, keepdims=True)


def as_row(column):
    same = iota((KB, KB), 0) == iota((KB, KB), 1)
    return jnp.sum(jnp.where(same, jnp.broadcast_to(column, (KB, KB)), 0.0), axis=0, keepdims=True)


def group_mask():
    return iota((KB, LANES), 0) // MODES == iota((KB, LANES), 1) // CH


def by_channel(column):
    spread = jnp.where(group_mask(), jnp.broadcast_to(column, (KB, LANES)), 0.0)
    return jnp.sum(spread.reshape(GPB, MODES, LANES), axis=0)


def short_conv(x, before, taps):
    sub = iota((8, x.shape[1]), 0)
    older, newer = before[0:1, :], before[1:2, :]
    one = pltpu.roll(x, 1, 0)
    two = pltpu.roll(x, 2, 0)
    one_top = jnp.where(sub == 0, newer, one[:8])
    two_top = jnp.where(sub == 0, older, jnp.where(sub == 1, newer, two[:8]))
    one = jnp.concatenate([one_top, one[8:]], axis=0)
    two = jnp.concatenate([two_top, two[8:]], axis=0)
    return taps[0] * x + taps[1] * one + taps[2] * two


def main_kernel(
    nz,
    ny,
    tokens,
    blocks,
    proj_hbm,
    resid_hbm,
    weight_hbm,
    rates_hbm,
    residues_hbm,
    skip_hbm,
    summed_ref,
    inv_ref,
    weight_ref,
    rates_ref,
    residues_ref,
    skip_ref,
    proj,
    resid,
    halo_out,
    halo_in,
    weights,
    p_buf,
    q_buf,
    base_buf,
    e_buf,
    f_buf,
    h_buf,
    edge_buf,
    edge_in,
    s_buf,
    rs_buf,
    b_buf,
    c_buf,
    z_buf,
    x_out,
    x_buf,
    sq_acc,
    sq_out,
    sq_buf,
    load_sem,
    halo_sem,
    edge_send,
    edge_recv,
    rs_send,
    rs_recv,
    ready,
    f_send,
    z_send,
    z_recv,
    x_send,
    x_recv,
    y_send,
    y_recv,
):
    width = blocks * LANES
    ctx = lax.axis_index("ctx")
    y = lax.axis_index("fsdp")
    z = ctx // ROW
    me = ctx % ROW
    last = nz * ROW - 1
    loads = [
        pltpu.make_async_copy(proj_hbm.at[c], proj.at[c], load_sem.at[c]) for c in (1, 2, 0)
    ] + [pltpu.make_async_copy(resid_hbm, resid, load_sem.at[3])]
    small = [
        pltpu.make_async_copy(src, dst, load_sem.at[4 + k])
        for k, (src, dst) in enumerate(
            (
                (rates_hbm, rates_ref),
                (residues_hbm, residues_ref),
                (weight_hbm, weight_ref),
                (skip_hbm, skip_ref),
            )
        )
    ]
    for load in small + loads[:2]:
        load.start()
    barrier = pltpu.get_barrier_semaphore()

    def hello(**where):
        pl.semaphore_signal(barrier, inc=1, device_id=where, device_id_type=MESH)

    for k in range(1, REACH + 1):

        @pl.when(z >= k)
        def _():
            hello(ctx=ctx - k * ROW)

    for k in range(1, ROW):
        hello(ctx=z * ROW + (me + k) % ROW)
    for k in range(1, ny):
        hello(fsdp=(y + k) % ny)

    @pl.when((z > 0) & (me < ROW - 1))
    def _():
        hello(ctx=z * ROW - 1)

    far = [k for k in range(nz - 1, NEAR, -1)]

    @pl.when(z == 0)
    def _():
        for k in far:
            hello(ctx=me + k * ROW)

    for load in small:
        load.wait()
    weights[...] = weight_ref[...].astype(F32)
    lag = (tokens - 1 - iota((1, tokens), 1)).astype(F32)

    def fill_states(block, carry):
        rate = mode_column(rates_ref, block)
        residue = mode_column(residues_ref, block)
        decay = jnp.exp(-rate * lag)
        high, low = split(decay)
        e_buf[block, pl.ds(0, KB), :] = high
        e_buf[block, pl.ds(KB, KB), :] = low
        edge_buf[block, 0] = by_channel(decay[:, 0:1])
        edge_buf[block, 1] = by_channel(decay[:, 1:2])
        h_buf[block] = jnp.sum((residue * decay).reshape(GPB, MODES, tokens), axis=1)
        return carry

    lax.fori_loop(0, blocks, fill_states, 0, unroll=True)
    for load in loads[:2]:
        load.wait()
    for load in loads[2:]:
        load.start()

    def taps_of(c, cols):
        return [weights[tap, c : c + 1, cols] for tap in range(3)]

    def states(block, carry):
        cols = pl.ds(pl.multiple_of(block * LANES, LANES), LANES)
        none = jnp.zeros((2, LANES), F32)
        key = short_conv(proj[1, :, cols].astype(F32), none, taps_of(1, cols))
        product = key * short_conv(proj[2, :, cols].astype(F32), none, taps_of(2, cols))
        top = jnp.where(iota((8, LANES), 0) < 2, 0.0, product[:8])
        product = jnp.concatenate([top, product[8:]], axis=0).astype(BF16)
        p_buf[block] = product
        both = jnp.dot(e_buf[block], product, preferred_element_type=F32)
        total = jnp.where(group_mask(), both[:KB] + both[KB:], 0.0)
        s_buf[block, pl.ds(0, MODES), :] = jnp.sum(total.reshape(GPB, MODES, LANES), axis=0)
        return carry

    for c in (1, 2):
        tail = proj[c, tokens - 16 :, :].astype(F32)[14:16]
        head = proj[c, :16, :].astype(F32)[:2]
        halo_out[c] = tail
        for block in range(blocks):
            mine = slice(block * LANES, (block + 1) * LANES)
            s_buf[block, pl.ds(MODES + 2 * c - 2, 2), :] = tail[:, mine]
            s_buf[block, pl.ds(MODES + 2 * c + 2, 2), :] = head[:, mine]
    lax.fori_loop(0, blocks, states, 0, unroll=True)
    loads[2].wait()
    halo_out[0] = proj[0, tokens - 16 :, :].astype(F32)[14:16]

    reach = jnp.minimum(nz - 1 - z, REACH)
    fan = jnp.minimum(reach, 1) * (me // (ROW - 1)) * (ROW - 1)
    distant = jnp.minimum(z // (NEAR + 1), 1)
    pl.semaphore_wait(barrier, ROW - 1 + ny - 1 + reach + fan + distant)

    @pl.when(distant == 1)
    def _():
        pl.semaphore_signal(ready.at[z], inc=1, device_id={"ctx": me}, device_id_type=MESH)

    def rs_copy(k, slot, target):
        return pltpu.make_async_remote_copy(
            src_ref=s_buf.at[target],
            dst_ref=rs_buf.at[slot],
            send_sem=rs_send.at[k],
            recv_sem=rs_recv.at[slot],
            device_id={"ctx": z * ROW + target},
            device_id_type=MESH,
        )

    def edge_copy(k):
        return pltpu.make_async_remote_copy(
            src_ref=s_buf.at[k, pl.ds(MODES, 8)],
            dst_ref=edge_in,
            send_sem=edge_send.at[k],
            recv_sem=edge_recv,
            device_id={"ctx": jnp.minimum(z * ROW + ROW + k, last)},
            device_id_type=MESH,
        )

    feeds = (me == ROW - 1) & (z < nz - 1)

    @pl.when(feeds)
    def _():
        for k in range(ROW):
            edge_copy(k).start()

    for k in range(1, ROW):
        rs_copy(k, me, (me + k) % ROW).start()
    rs_buf[me] = s_buf[me]

    def halo_copy():
        return pltpu.make_async_remote_copy(
            src_ref=halo_out,
            dst_ref=halo_in,
            send_sem=halo_sem.at[0],
            recv_sem=halo_sem.at[1],
            device_id={"ctx": jnp.minimum(ctx + 1, last)},
            device_id_type=MESH,
        )

    @pl.when(ctx < last)
    def _():
        halo_copy().start()

    @pl.when(ctx == 0)
    def _():
        halo_in[...] = jnp.zeros_like(halo_in)

    @pl.when(ctx > 0)
    def _():
        halo_copy().wait_recv()

    def filtered(c, cols):
        return short_conv(proj[c, :, cols].astype(F32), halo_in[c, :, cols], taps_of(c, cols))

    def first_rows(c):
        every = slice(None)
        return short_conv(proj[c, :16, :].astype(F32), halo_in[c], taps_of(c, every))

    product_top = (first_rows(1) * first_rows(2)).astype(BF16)
    for block in range(blocks):
        p_buf[block, pl.ds(0, 16), :] = product_top[:, block * LANES : (block + 1) * LANES]

    loads[3].wait()
    lag_next = (iota((tokens, 1), 0) + 1).astype(F32)

    def local(block, carry):
        cols = pl.ds(pl.multiple_of(block * LANES, LANES), LANES)
        rate = as_row(mode_column(rates_ref, block))
        residue = as_row(mode_column(residues_ref, block))
        high, low = split(residue * jnp.exp(-rate * lag_next))
        f_buf[block, :, pl.ds(0, KB)] = high
        f_buf[block, :, pl.ds(KB, KB)] = low
        product = p_buf[block]
        half = tokens // 2
        lane_group = iota((tokens, LANES), 1) // CH
        causal = iota((half, half), 1) <= iota((half, half), 0)
        taps = h_buf[block]
        total = jnp.zeros((tokens, LANES), F32)
        for g in range(GPB):
            row = jnp.broadcast_to(taps[g : g + 1], (half, tokens))
            rolled = pltpu.roll(row, half + 1, 1, stride=1, stride_axis=0)
            far = rolled[:, :half].astype(BF16)
            near = jnp.where(causal, rolled[:, half:], 0.0).astype(BF16)
            matrix = jnp.concatenate(
                [
                    jnp.concatenate([near, jnp.zeros_like(near)], axis=1),
                    jnp.concatenate([far, near], axis=1),
                ],
                axis=0,
            )
            part = jnp.where(lane_group == g, product, jnp.zeros_like(product))
            total = total + jnp.dot(matrix, part, preferred_element_type=F32)
        query = filtered(0, cols)
        q_buf[block] = query
        wide = product.astype(F32)
        base_buf[block] = resid[:, cols].astype(F32) + query * (total + skip_ref[:, cols] * wide)
        return carry

    lax.fori_loop(0, LOCAL_A, local, 0, unroll=True)

    rate = by_channel(mode_column(rates_ref, me))
    one_block = jnp.exp(-rate * float(tokens))
    one_row = jnp.exp(-rate * float(tokens * ROW))
    for k in range(1, ROW):
        source = (me + ROW - k) % ROW
        rs_copy(k, source, me).wait_recv()

    @pl.when(z == 0)
    def _():
        edge_in[...] = jnp.zeros_like(edge_in)

    @pl.when(z > 0)
    def _():
        edge_copy(0).wait_recv()

    mine = pl.ds(pl.multiple_of(me * LANES, LANES), LANES)
    key_taps, value_taps = taps_of(1, mine), taps_of(2, mine)

    def first_two(before, at, taps):
        now = rs_buf[at, pl.ds(MODES + 4, 4), :]
        out = []
        for c, w in enumerate(taps):
            older = before[2 * c : 2 * c + 1]
            newer = before[2 * c + 1 : 2 * c + 2]
            first = now[2 * c : 2 * c + 1]
            second = now[2 * c + 1 : 2 * c + 2]
            out.append(
                (
                    w[0] * first + w[1] * newer + w[2] * older,
                    w[0] * second + w[1] * first + w[2] * newer,
                )
            )
        return [(out[0][i] * out[1][i]).astype(BF16).astype(F32) for i in range(2)]

    prefixes = [jnp.zeros((MODES, LANES), F32)]
    for i in range(ROW):
        before = edge_in[:4, :] if i == 0 else rs_buf[i - 1, pl.ds(MODES, 4), :]
        one, two = first_two(before, i, (key_taps, value_taps))
        state = rs_buf[i, pl.ds(0, MODES), :] + edge_buf[me, 0] * one + edge_buf[me, 1] * two
        prefixes.append(one_block * prefixes[-1] + state)
    b_buf[0] = prefixes[ROW]

    def z_copy(k):
        return pltpu.make_async_remote_copy(
            src_ref=b_buf.at[k // REACH],
            dst_ref=z_buf.at[k],
            send_sem=z_send.at[k],
            recv_sem=z_recv.at[k],
            device_id={"ctx": jnp.minimum(ctx + k * ROW, last)},
            device_id_type=MESH,
        )

    def first_copy(k):
        return pltpu.make_async_remote_copy(
            src_ref=b_buf.at[0],
            dst_ref=z_buf.at[0],
            send_sem=f_send.at[k],
            recv_sem=z_recv.at[0],
            device_id={"ctx": jnp.minimum(me + k * ROW, last)},
            device_id_type=MESH,
        )

    def relay_copy():
        return pltpu.make_async_remote_copy(
            src_ref=z_buf.at[0],
            dst_ref=z_buf.at[0],
            send_sem=z_send.at[0],
            recv_sem=z_recv.at[0],
            device_id={"ctx": jnp.minimum(ctx + REACH * ROW, last)},
            device_id_type=MESH,
        )

    @pl.when(z == 0)
    def _():
        for k in range(1, min(REACH, nz - 1) + 1):
            first_copy(k).start()

    for k in range(1, REACH):

        @pl.when((z > 0) & (z + k < nz))
        def _():
            z_copy(k).start()

    lax.fori_loop(LOCAL_A, LOCAL_B, local, 0, unroll=True)

    c_buf[...] = jnp.zeros_like(c_buf)
    for k in range(REACH, 0, -1):

        @pl.when(k < z)
        def _():
            z_copy(k).wait_recv()
            c_buf[...] = one_row * c_buf[...] + z_buf[k]

    chain = c_buf[...]
    b_buf[1] = one_row * chain + prefixes[ROW]

    @pl.when((z > 0) & (z + REACH < nz))
    def _():
        z_copy(REACH).start()

    @pl.when(z > 0)
    def _():
        first_copy(1).wait_recv()

    @pl.when((z > 0) & (z + REACH <= min(NEAR, nz - 1)))
    def _():
        relay_copy().start()

    @pl.when(z > 0)
    def _():
        weight = jnp.exp(-rate * ((z - 1) * (tokens * ROW)).astype(F32))
        c_buf[...] = chain + weight * z_buf[0]

    entering = c_buf[...]

    for i in range(ROW):
        value = jnp.exp(-rate * float(tokens * i)) * entering + prefixes[i]
        x_out[i] = value.astype(x_out.dtype)

    def x_copy(k, slot, target):
        return pltpu.make_async_remote_copy(
            src_ref=x_out.at[target],
            dst_ref=x_buf.at[slot],
            send_sem=x_send.at[k],
            recv_sem=x_recv.at[slot],
            device_id={"ctx": z * ROW + target},
            device_id_type=MESH,
        )

    for k in range(1, ROW):
        x_copy(k, me, (me + k) % ROW).start()
    x_buf[me] = x_out[me]
    lax.fori_loop(LOCAL_B, blocks, local, 0, unroll=True)
    @pl.when(z == 0)
    def _():
        for k in far:
            pl.semaphore_wait(ready.at[k], 1)
            first_copy(k).start()

    sq_acc[...] = jnp.zeros_like(sq_acc)
    for k in range(1, ROW):
        x_copy(k, (me + ROW - k) % ROW, me).wait_recv()

    def finish(block, carry):
        cols = pl.ds(pl.multiple_of(block * LANES, LANES), LANES)
        state = jnp.broadcast_to(x_buf[block].astype(F32)[None], (GPB, MODES, LANES)).reshape(KB, LANES)
        state = jnp.where(group_mask(), state, 0.0).astype(BF16)
        carried = jnp.dot(
            f_buf[block], jnp.concatenate([state, state], axis=0), preferred_element_type=F32
        )
        summed = base_buf[block] + q_buf[block] * carried
        summed_ref[:, cols] = summed
        sq_acc[...] += summed * summed
        return carry

    lax.fori_loop(0, blocks, finish, 0, unroll=True)
    ones = jnp.ones((8, LANES), BF16)
    contract = (((1,), (1,)), ((), ()))
    high, low = split(sq_acc[...])
    squares = lax.dot_general(ones, high, contract, preferred_element_type=F32) + lax.dot_general(
        ones, low, contract, preferred_element_type=F32
    )
    sq_out[...] = squares[:1]

    def y_copy(k, slot, target):
        return pltpu.make_async_remote_copy(
            src_ref=sq_out,
            dst_ref=sq_buf.at[slot],
            send_sem=y_send.at[k],
            recv_sem=y_recv.at[slot],
            device_id={"fsdp": target},
            device_id_type=MESH,
        )

    for k in range(1, ny):
        y_copy(k, y, (y + k) % ny).start()
    sq_buf[y] = sq_out[...]

    for k in range(1, ny):
        y_copy(k, (y + ny - k) % ny, y).wait_recv()
    total = sq_buf[0]
    for k in range(1, ny):
        total = total + sq_buf[k]
    scale = lax.rsqrt(total / float(width * ny) + 1e-05)
    inv_ref[...] = jnp.transpose(jnp.broadcast_to(scale, (LANES, tokens)))

    @pl.when(ctx < last)
    def _():
        halo_copy().wait_send()

    @pl.when(feeds)
    def _():
        for k in range(ROW):
            edge_copy(k).wait_send()

    for k in range(1, ROW):
        rs_copy(k, me, (me + k) % ROW).wait_send()
        x_copy(k, me, (me + k) % ROW).wait_send()
    for k in range(1, REACH + 1):

        @pl.when((z > 0) & (z + k < nz))
        def _():
            z_copy(k).wait_send()

    @pl.when((z > 0) & (z + REACH <= min(NEAR, nz - 1)))
    def _():
        relay_copy().wait_send()

    @pl.when(z == 0)
    def _():
        for k in list(range(1, min(REACH, nz - 1) + 1)) + far:
            first_copy(k).wait_send()

    for k in range(1, ny):
        y_copy(k, y, (y + k) % ny).wait_send()


def per_device(nz, ny, projected, short_weight, rates, residues, skip, residual, gain):
    tokens, width = residual.shape
    blocks = width // LANES
    vmem = pl.BlockSpec(memory_space=pltpu.VMEM)
    hbm = pl.BlockSpec(memory_space=pltpu.HBM)
    dma = pltpu.SemaphoreType.DMA
    summed, inv = pl.pallas_call(
        functools.partial(main_kernel, nz, ny, tokens, blocks),
        out_shape=(
            jax.ShapeDtypeStruct((tokens, width), F32),
            jax.ShapeDtypeStruct((tokens, LANES), F32),
        ),
        in_specs=[hbm] * 6,
        out_specs=(vmem, vmem),
        scratch_shapes=[
            pltpu.VMEM(short_weight.shape, BF16),
            pltpu.VMEM((MODES, width // CH), F32),
            pltpu.VMEM((MODES, width // CH), F32),
            pltpu.VMEM((1, width), F32),
            pltpu.VMEM((3, tokens, width), BF16),
            pltpu.VMEM((tokens, width), BF16),
            pltpu.VMEM((3, 2, width), F32),
            pltpu.VMEM((3, 2, width), F32),
            pltpu.VMEM((3, 3, width), F32),
            pltpu.VMEM((blocks, tokens, LANES), BF16),
            pltpu.VMEM((blocks, tokens, LANES), F32),
            pltpu.VMEM((blocks, tokens, LANES), F32),
            pltpu.VMEM((blocks, 2 * KB, tokens), BF16),
            pltpu.VMEM((blocks, tokens, 2 * KB), BF16),
            pltpu.VMEM((blocks, GPB, tokens), F32),
            pltpu.VMEM((blocks, 2, MODES, LANES), F32),
            pltpu.VMEM((8, LANES), F32),
            pltpu.VMEM((ROW, SENT, LANES), F32),
            pltpu.VMEM((ROW, SENT, LANES), F32),
            pltpu.VMEM((2, MODES, LANES), F32),
            pltpu.VMEM((MODES, LANES), F32),
            pltpu.VMEM((REACH + 1, MODES, LANES), F32),
            pltpu.VMEM((ROW, MODES, LANES), BF16),
            pltpu.VMEM((ROW, MODES, LANES), BF16),
            pltpu.VMEM((tokens, LANES), F32),
            pltpu.VMEM((1, tokens), F32),
            pltpu.VMEM((ny, 1, tokens), F32),
            dma((8,)),
            dma((2,)),
            dma((ROW,)),
            dma,
            dma((ROW,)),
            dma((ROW,)),
            pltpu.SemaphoreType.REGULAR((nz,)),
            dma((nz,)),
            dma((REACH + 1,)),
            dma((REACH + 1,)),
            dma((ROW,)),
            dma((ROW,)),
            dma((ny,)),
            dma((ny,)),
        ],
        compiler_params=pltpu.CompilerParams(
            collective_id=0, has_side_effects=True, vmem_limit_bytes=40 << 20
        ),
        name="scan_conv",
    )(
        *[
            pltpu.with_memory_space_constraint(operand, pltpu.HBM)
            for operand in (
                projected,
                residual,
                short_weight,
                rates.T,
                residues.T,
                skip.reshape(1, width),
            )
        ]
    )
    new_residual = summed.astype(BF16)
    normed = (summed * inv[:, :1] * gain[None, :]).astype(BF16)
    return new_residual, normed


def solution(mesh):
    nz = mesh.shape["ctx"] // ROW
    ny = mesh.shape["fsdp"]
    return jax.shard_map(
        functools.partial(per_device, nz, ny),
        mesh=mesh,
        in_specs=(
            P(None, "ctx", "fsdp"),
            P(None, None, "fsdp"),
            P("fsdp", None),
            P("fsdp", None),
            P("fsdp"),
            P("ctx", "fsdp"),
            P("fsdp"),
        ),
        out_specs=(P("ctx", "fsdp"), P("ctx", "fsdp")),
        check_vma=False,
    )
```

```python
import functools

import jax
import jax.numpy as jnp
from jax import lax
from jax.experimental import pallas as pl
from jax.experimental.pallas import tpu as pltpu
from jax.sharding import PartitionSpec as P

CH = 16
MODES = 16
LANES = 128
GPB = LANES // CH
KB = GPB * MODES
ROW = 8
F32 = jnp.float32
BF16 = jnp.bfloat16
MESH = pl.DeviceIdType.MESH
REACH = 3
CHIPS = ROW // 2
RING = [(step, core) for step in (2, 1, 3) for core in (0, 1)]
NEAR = 7
LOCAL_A = 1
LOCAL_B = 4
SENT = MODES + 8


def iota(shape, dim):
    return lax.broadcasted_iota(jnp.int32, shape, dim)


def split(value):
    high = value.astype(BF16)
    return high, (value - high.astype(F32)).astype(BF16)


def mode_column(ref, block):
    groups = ref.shape[1]
    spread = jnp.broadcast_to(ref[...][None], (GPB, MODES, groups)).reshape(KB, groups)
    own = iota((KB, groups), 1) == block * GPB + iota((KB, groups), 0) // MODES
    return jnp.sum(jnp.where(own, spread, 0.0), axis=1, keepdims=True)


def as_row(column):
    same = iota((KB, KB), 0) == iota((KB, KB), 1)
    return jnp.sum(jnp.where(same, jnp.broadcast_to(column, (KB, KB)), 0.0), axis=0, keepdims=True)


def group_mask():
    return iota((KB, LANES), 0) // MODES == iota((KB, LANES), 1) // CH


def by_channel(column):
    spread = jnp.where(group_mask(), jnp.broadcast_to(column, (KB, LANES)), 0.0)
    return jnp.sum(spread.reshape(GPB, MODES, LANES), axis=0)


def short_conv(x, before, taps):
    sub = iota((8, x.shape[1]), 0)
    older, newer = before[0:1, :], before[1:2, :]
    one = pltpu.roll(x, 1, 0)
    two = pltpu.roll(x, 2, 0)
    one_top = jnp.where(sub == 0, newer, one[:8])
    two_top = jnp.where(sub == 0, older, jnp.where(sub == 1, newer, two[:8]))
    one = jnp.concatenate([one_top, one[8:]], axis=0)
    two = jnp.concatenate([two_top, two[8:]], axis=0)
    return taps[0] * x + taps[1] * one + taps[2] * two


def main_kernel(
    nz,
    ny,
    tokens,
    blocks,
    proj_hbm,
    resid_hbm,
    weight_hbm,
    rates_hbm,
    residues_hbm,
    skip_hbm,
    summed_ref,
    inv_ref,
    weight_ref,
    rates_ref,
    residues_ref,
    skip_ref,
    proj,
    resid,
    halo_out,
    halo_in,
    weights,
    p_buf,
    q_buf,
    base_buf,
    e_buf,
    f_buf,
    h_buf,
    edge_buf,
    edge_in,
    s_buf,
    rs_buf,
    b_buf,
    c_buf,
    z_buf,
    x_out,
    x_buf,
    sq_out,
    sq_buf,
    load_sem,
    halo_sem,
    edge_send,
    edge_recv,
    rs_send,
    rs_recv,
    ready,
    f_send,
    z_send,
    z_recv,
    x_send,
    x_recv,
    y_send,
    y_recv,
):
    width = blocks * LANES
    ctx = lax.axis_index("ctx")
    y = lax.axis_index("fsdp")
    z = ctx // ROW
    me = ctx % ROW
    last = nz * ROW - 1
    partner = me + 1 - 2 * (me % 2)
    peers = [((me // 2 + step) % CHIPS) * 2 + core for step, core in RING] + [partner]
    ring = sorted(range(1, ny), key=lambda k: -min(k, ny - k))
    halves = [pl.ds(h * (width // 2), width // 2) for h in range(2)]
    loads = [
        pltpu.make_async_copy(
            proj_hbm.at[c, :, part], proj.at[c, :, part], load_sem.at[8 + 2 * h + c - 1]
        )
        for h, part in enumerate(halves)
        for c in (1, 2)
    ] + [
        pltpu.make_async_copy(proj_hbm.at[0], proj.at[0], load_sem.at[0]),
        pltpu.make_async_copy(resid_hbm, resid, load_sem.at[3]),
    ]
    small = [
        pltpu.make_async_copy(src, dst, load_sem.at[4 + k])
        for k, (src, dst) in enumerate(
            (
                (rates_hbm, rates_ref),
                (residues_hbm, residues_ref),
                (weight_hbm, weight_ref),
                (skip_hbm, skip_ref),
            )
        )
    ]
    for load in small + loads[:4]:
        load.start()
    barrier = pltpu.get_barrier_semaphore()

    def hello(**where):
        pl.semaphore_signal(barrier, inc=1, device_id=where, device_id_type=MESH)

    for k in range(1, REACH + 1):

        @pl.when(z >= k)
        def _():
            hello(ctx=ctx - k * ROW)

    for k in range(1, ROW):
        hello(ctx=z * ROW + (me + k) % ROW)
    for k in range(1, ny):
        hello(fsdp=(y + k) % ny)

    @pl.when((z > 0) & (me < ROW - 1))
    def _():
        hello(ctx=z * ROW - 1)

    far = [k for k in range(nz - 1, NEAR, -1)]

    @pl.when(z == 0)
    def _():
        for k in far:
            hello(ctx=me + k * ROW)

    for load in small:
        load.wait()
    weights[...] = weight_ref[...].astype(F32)
    lag = (tokens - 1 - iota((1, tokens), 1)).astype(F32)

    def fill_states(block, carry):
        rate = mode_column(rates_ref, block)
        residue = mode_column(residues_ref, block)
        decay = jnp.exp(-rate * lag)
        high, low = split(decay)
        e_buf[block, pl.ds(0, KB), :] = high
        e_buf[block, pl.ds(KB, KB), :] = low
        edge_buf[block, 0] = by_channel(decay[:, 0:1])
        edge_buf[block, 1] = by_channel(decay[:, 1:2])
        h_buf[block] = jnp.sum((residue * decay).reshape(GPB, MODES, tokens), axis=1)
        return carry

    lax.fori_loop(0, blocks, fill_states, 0, unroll=True)
    for load in loads[:2]:
        load.wait()

    def taps_of(c, cols):
        return [weights[tap, c : c + 1, cols] for tap in range(3)]

    def states(block, carry):
        cols = pl.ds(pl.multiple_of(block * LANES, LANES), LANES)
        none = jnp.zeros((2, LANES), F32)
        key = short_conv(proj[1, :, cols].astype(F32), none, taps_of(1, cols))
        product = key * short_conv(proj[2, :, cols].astype(F32), none, taps_of(2, cols))
        top = jnp.where(iota((8, LANES), 0) < 2, 0.0, product[:8])
        product = jnp.concatenate([top, product[8:]], axis=0).astype(BF16)
        p_buf[block] = product
        both = jnp.dot(e_buf[block], product, preferred_element_type=F32)
        total = jnp.where(group_mask(), both[:KB] + both[KB:], 0.0)
        s_buf[block, pl.ds(0, MODES), :] = jnp.sum(total.reshape(GPB, MODES, LANES), axis=0)
        return carry

    lax.fori_loop(0, blocks // 2, states, 0, unroll=True)
    for load in loads[2:4]:
        load.wait()
    for load in loads[4:]:
        load.start()
    for c in (1, 2):
        tail = proj[c, tokens - 16 :, :].astype(F32)[14:16]
        head = proj[c, :16, :].astype(F32)[:2]
        halo_out[c] = tail
        for block in range(blocks):
            mine = slice(block * LANES, (block + 1) * LANES)
            s_buf[block, pl.ds(MODES + 2 * c - 2, 2), :] = tail[:, mine]
            s_buf[block, pl.ds(MODES + 2 * c + 2, 2), :] = head[:, mine]
    lax.fori_loop(blocks // 2, blocks, states, 0, unroll=True)
    loads[4].wait()
    halo_out[0] = proj[0, tokens - 16 :, :].astype(F32)[14:16]

    reach = jnp.minimum(nz - 1 - z, REACH)
    fan = jnp.minimum(reach, 1) * (me // (ROW - 1)) * (ROW - 1)
    distant = jnp.minimum(z // (NEAR + 1), 1)
    pl.semaphore_wait(barrier, ROW - 1 + ny - 1 + reach + fan + distant)

    @pl.when(distant == 1)
    def _():
        pl.semaphore_signal(ready.at[z], inc=1, device_id={"ctx": me}, device_id_type=MESH)

    def rs_copy(k, slot, target):
        return pltpu.make_async_remote_copy(
            src_ref=s_buf.at[target],
            dst_ref=rs_buf.at[slot],
            send_sem=rs_send.at[k],
            recv_sem=rs_recv.at[slot],
            device_id={"ctx": z * ROW + target},
            device_id_type=MESH,
        )

    def edge_copy(k):
        return pltpu.make_async_remote_copy(
            src_ref=s_buf.at[k, pl.ds(MODES, 8)],
            dst_ref=edge_in,
            send_sem=edge_send.at[k],
            recv_sem=edge_recv,
            device_id={"ctx": jnp.minimum(z * ROW + ROW + k, last)},
            device_id_type=MESH,
        )

    feeds = (me == ROW - 1) & (z < nz - 1)

    @pl.when(feeds)
    def _():
        for k in range(ROW):
            edge_copy(k).start()

    for k, peer in enumerate(peers):
        rs_copy(k, me, peer).start()
    rs_buf[me] = s_buf[me]

    def halo_copy():
        return pltpu.make_async_remote_copy(
            src_ref=halo_out,
            dst_ref=halo_in,
            send_sem=halo_sem.at[0],
            recv_sem=halo_sem.at[1],
            device_id={"ctx": jnp.minimum(ctx + 1, last)},
            device_id_type=MESH,
        )

    @pl.when(ctx < last)
    def _():
        halo_copy().start()

    @pl.when(ctx == 0)
    def _():
        halo_in[...] = jnp.zeros_like(halo_in)

    @pl.when(ctx > 0)
    def _():
        halo_copy().wait_recv()

    def filtered(c, cols):
        return short_conv(proj[c, :, cols].astype(F32), halo_in[c, :, cols], taps_of(c, cols))

    def first_rows(c):
        every = slice(None)
        return short_conv(proj[c, :16, :].astype(F32), halo_in[c], taps_of(c, every))

    product_top = (first_rows(1) * first_rows(2)).astype(BF16)
    for block in range(blocks):
        p_buf[block, pl.ds(0, 16), :] = product_top[:, block * LANES : (block + 1) * LANES]

    loads[5].wait()
    lag_next = (iota((tokens, 1), 0) + 1).astype(F32)

    def local(block, carry):
        cols = pl.ds(pl.multiple_of(block * LANES, LANES), LANES)
        rate = as_row(mode_column(rates_ref, block))
        residue = as_row(mode_column(residues_ref, block))
        high, low = split(residue * jnp.exp(-rate * lag_next))
        f_buf[block, :, pl.ds(0, KB)] = high
        f_buf[block, :, pl.ds(KB, KB)] = low
        product = p_buf[block]
        half = tokens // 2
        lane_group = iota((tokens, LANES), 1) // CH
        causal = iota((half, half), 1) <= iota((half, half), 0)
        taps = h_buf[block]
        total = jnp.zeros((tokens, LANES), F32)
        for g in range(GPB):
            row = jnp.broadcast_to(taps[g : g + 1], (half, tokens))
            rolled = pltpu.roll(row, half + 1, 1, stride=1, stride_axis=0)
            far = rolled[:, :half].astype(BF16)
            near = jnp.where(causal, rolled[:, half:], 0.0).astype(BF16)
            matrix = jnp.concatenate(
                [
                    jnp.concatenate([near, jnp.zeros_like(near)], axis=1),
                    jnp.concatenate([far, near], axis=1),
                ],
                axis=0,
            )
            part = jnp.where(lane_group == g, product, jnp.zeros_like(product))
            total = total + jnp.dot(matrix, part, preferred_element_type=F32)
        query = filtered(0, cols)
        q_buf[block] = query
        wide = product.astype(F32)
        base_buf[block] = resid[:, cols].astype(F32) + query * (total + skip_ref[:, cols] * wide)
        return carry

    lax.fori_loop(0, LOCAL_A, local, 0, unroll=True)

    rate = by_channel(mode_column(rates_ref, me))
    one_block = jnp.exp(-rate * float(tokens))
    one_row = jnp.exp(-rate * float(tokens * ROW))
    for k, peer in enumerate(peers):
        rs_copy(k, peer, me).wait_recv()

    @pl.when(z == 0)
    def _():
        edge_in[...] = jnp.zeros_like(edge_in)

    @pl.when(z > 0)
    def _():
        edge_copy(0).wait_recv()

    mine = pl.ds(pl.multiple_of(me * LANES, LANES), LANES)
    key_taps, value_taps = taps_of(1, mine), taps_of(2, mine)

    def first_two(before, at, taps):
        now = rs_buf[at, pl.ds(MODES + 4, 4), :]
        out = []
        for c, w in enumerate(taps):
            older = before[2 * c : 2 * c + 1]
            newer = before[2 * c + 1 : 2 * c + 2]
            first = now[2 * c : 2 * c + 1]
            second = now[2 * c + 1 : 2 * c + 2]
            out.append(
                (
                    w[0] * first + w[1] * newer + w[2] * older,
                    w[0] * second + w[1] * first + w[2] * newer,
                )
            )
        return [(out[0][i] * out[1][i]).astype(BF16).astype(F32) for i in range(2)]

    prefixes = [jnp.zeros((MODES, LANES), F32)]
    for i in range(ROW):
        before = edge_in[:4, :] if i == 0 else rs_buf[i - 1, pl.ds(MODES, 4), :]
        one, two = first_two(before, i, (key_taps, value_taps))
        state = rs_buf[i, pl.ds(0, MODES), :] + edge_buf[me, 0] * one + edge_buf[me, 1] * two
        prefixes.append(one_block * prefixes[-1] + state)
    b_buf[0] = prefixes[ROW]

    def z_copy(k):
        return pltpu.make_async_remote_copy(
            src_ref=b_buf.at[k // REACH],
            dst_ref=z_buf.at[k],
            send_sem=z_send.at[k],
            recv_sem=z_recv.at[k],
            device_id={"ctx": jnp.minimum(ctx + k * ROW, last)},
            device_id_type=MESH,
        )

    def first_copy(k):
        return pltpu.make_async_remote_copy(
            src_ref=b_buf.at[0],
            dst_ref=z_buf.at[0],
            send_sem=f_send.at[k],
            recv_sem=z_recv.at[0],
            device_id={"ctx": jnp.minimum(me + k * ROW, last)},
            device_id_type=MESH,
        )

    def relay_copy():
        return pltpu.make_async_remote_copy(
            src_ref=z_buf.at[0],
            dst_ref=z_buf.at[0],
            send_sem=z_send.at[0],
            recv_sem=z_recv.at[0],
            device_id={"ctx": jnp.minimum(ctx + REACH * ROW, last)},
            device_id_type=MESH,
        )

    @pl.when(z == 0)
    def _():
        for k in range(1, min(REACH, nz - 1) + 1):
            first_copy(k).start()

    for k in range(1, REACH):

        @pl.when((z > 0) & (z + k < nz))
        def _():
            z_copy(k).start()

    lax.fori_loop(LOCAL_A, LOCAL_B, local, 0, unroll=True)

    c_buf[...] = jnp.zeros_like(c_buf)
    for k in range(REACH, 0, -1):

        @pl.when(k < z)
        def _():
            z_copy(k).wait_recv()
            c_buf[...] = one_row * c_buf[...] + z_buf[k]

    chain = c_buf[...]
    b_buf[1] = one_row * chain + prefixes[ROW]

    @pl.when((z > 0) & (z + REACH < nz))
    def _():
        z_copy(REACH).start()

    @pl.when(z > 0)
    def _():
        first_copy(1).wait_recv()

    @pl.when((z > 0) & (z + REACH <= min(NEAR, nz - 1)))
    def _():
        relay_copy().start()

    @pl.when(z > 0)
    def _():
        weight = jnp.exp(-rate * ((z - 1) * (tokens * ROW)).astype(F32))
        c_buf[...] = chain + weight * z_buf[0]

    entering = c_buf[...]

    for i in range(ROW):
        value = jnp.exp(-rate * float(tokens * i)) * entering + prefixes[i]
        x_out[i] = value.astype(x_out.dtype)

    def x_copy(k, slot, target):
        return pltpu.make_async_remote_copy(
            src_ref=x_out.at[target],
            dst_ref=x_buf.at[slot],
            send_sem=x_send.at[k],
            recv_sem=x_recv.at[slot],
            device_id={"ctx": z * ROW + target},
            device_id_type=MESH,
        )

    for k, peer in enumerate(peers):
        x_copy(k, me, peer).start()
    x_buf[me] = x_out[me]
    lax.fori_loop(LOCAL_B, blocks, local, 0, unroll=True)
    @pl.when(z == 0)
    def _():
        for k in far:
            pl.semaphore_wait(ready.at[k], 1)
            first_copy(k).start()


    def finish(block, carry):
        cols = pl.ds(pl.multiple_of(block * LANES, LANES), LANES)
        state = jnp.broadcast_to(x_buf[block].astype(F32)[None], (GPB, MODES, LANES)).reshape(KB, LANES)
        state = jnp.where(group_mask(), state, 0.0).astype(BF16)
        carried = jnp.dot(
            f_buf[block], jnp.concatenate([state, state], axis=0), preferred_element_type=F32
        )
        summed = base_buf[block] + q_buf[block] * carried
        summed_ref[:, cols] = summed
        return carry + summed * summed

    squared = finish(me, jnp.zeros((tokens, LANES), F32))
    for k, peer in reversed(list(enumerate(peers))):
        x_copy(k, peer, me).wait_recv()
        squared = finish(peer, squared)
    ones = jnp.ones((8, LANES), BF16)
    contract = (((1,), (1,)), ((), ()))
    high, low = split(squared)
    squares = lax.dot_general(ones, high, contract, preferred_element_type=F32) + lax.dot_general(
        ones, low, contract, preferred_element_type=F32
    )
    sq_out[...] = squares[:1]

    def y_copy(k, slot, target):
        return pltpu.make_async_remote_copy(
            src_ref=sq_out,
            dst_ref=sq_buf.at[slot],
            send_sem=y_send.at[k],
            recv_sem=y_recv.at[slot],
            device_id={"fsdp": target},
            device_id_type=MESH,
        )

    for k in ring:
        y_copy(k, y, (y + k) % ny).start()
    sq_buf[y] = sq_out[...]

    for k in range(1, ny):
        y_copy(k, (y + ny - k) % ny, y).wait_recv()
    total = sq_buf[0]
    for k in range(1, ny):
        total = total + sq_buf[k]
    scale = lax.rsqrt(total / float(width * ny) + 1e-05)
    inv_ref[...] = jnp.transpose(jnp.broadcast_to(scale, (LANES, tokens)))

    @pl.when(ctx < last)
    def _():
        halo_copy().wait_send()

    @pl.when(feeds)
    def _():
        for k in range(ROW):
            edge_copy(k).wait_send()

    for k, peer in enumerate(peers):
        rs_copy(k, me, peer).wait_send()
        x_copy(k, me, peer).wait_send()
    for k in range(1, REACH + 1):

        @pl.when((z > 0) & (z + k < nz))
        def _():
            z_copy(k).wait_send()

    @pl.when((z > 0) & (z + REACH <= min(NEAR, nz - 1)))
    def _():
        relay_copy().wait_send()

    @pl.when(z == 0)
    def _():
        for k in list(range(1, min(REACH, nz - 1) + 1)) + far:
            first_copy(k).wait_send()

    for k in range(1, ny):
        y_copy(k, y, (y + k) % ny).wait_send()


def per_device(nz, ny, projected, short_weight, rates, residues, skip, residual, gain):
    tokens, width = residual.shape
    blocks = width // LANES
    vmem = pl.BlockSpec(memory_space=pltpu.VMEM)
    hbm = pl.BlockSpec(memory_space=pltpu.HBM)
    dma = pltpu.SemaphoreType.DMA
    summed, inv = pl.pallas_call(
        functools.partial(main_kernel, nz, ny, tokens, blocks),
        out_shape=(
            jax.ShapeDtypeStruct((tokens, width), F32),
            jax.ShapeDtypeStruct((tokens, LANES), F32),
        ),
        in_specs=[hbm] * 6,
        out_specs=(vmem, vmem),
        scratch_shapes=[
            pltpu.VMEM(short_weight.shape, BF16),
            pltpu.VMEM((MODES, width // CH), F32),
            pltpu.VMEM((MODES, width // CH), F32),
            pltpu.VMEM((1, width), F32),
            pltpu.VMEM((3, tokens, width), BF16),
            pltpu.VMEM((tokens, width), BF16),
            pltpu.VMEM((3, 2, width), F32),
            pltpu.VMEM((3, 2, width), F32),
            pltpu.VMEM((3, 3, width), F32),
            pltpu.VMEM((blocks, tokens, LANES), BF16),
            pltpu.VMEM((blocks, tokens, LANES), F32),
            pltpu.VMEM((blocks, tokens, LANES), F32),
            pltpu.VMEM((blocks, 2 * KB, tokens), BF16),
            pltpu.VMEM((blocks, tokens, 2 * KB), BF16),
            pltpu.VMEM((blocks, GPB, tokens), F32),
            pltpu.VMEM((blocks, 2, MODES, LANES), F32),
            pltpu.VMEM((8, LANES), F32),
            pltpu.VMEM((ROW, SENT, LANES), F32),
            pltpu.VMEM((ROW, SENT, LANES), F32),
            pltpu.VMEM((2, MODES, LANES), F32),
            pltpu.VMEM((MODES, LANES), F32),
            pltpu.VMEM((REACH + 1, MODES, LANES), F32),
            pltpu.VMEM((ROW, MODES, LANES), BF16),
            pltpu.VMEM((ROW, MODES, LANES), BF16),
            pltpu.VMEM((1, tokens), F32),
            pltpu.VMEM((ny, 1, tokens), F32),
            dma((12,)),
            dma((2,)),
            dma((ROW,)),
            dma,
            dma((ROW,)),
            dma((ROW,)),
            pltpu.SemaphoreType.REGULAR((nz,)),
            dma((nz,)),
            dma((REACH + 1,)),
            dma((REACH + 1,)),
            dma((ROW,)),
            dma((ROW,)),
            dma((ny,)),
            dma((ny,)),
        ],
        compiler_params=pltpu.CompilerParams(
            collective_id=0, has_side_effects=True, vmem_limit_bytes=40 << 20
        ),
        name="scan_conv",
    )(
        *[
            pltpu.with_memory_space_constraint(operand, pltpu.HBM)
            for operand in (
                projected,
                residual,
                short_weight,
                rates.T,
                residues.T,
                skip.reshape(1, width),
            )
        ]
    )
    new_residual = summed.astype(BF16)
    normed = (summed * inv[:, :1] * gain[None, :]).astype(BF16)
    return new_residual, normed


def solution(mesh):
    nz = mesh.shape["ctx"] // ROW
    ny = mesh.shape["fsdp"]
    return jax.shard_map(
        functools.partial(per_device, nz, ny),
        mesh=mesh,
        in_specs=(
            P(None, "ctx", "fsdp"),
            P(None, None, "fsdp"),
            P("fsdp", None),
            P("fsdp", None),
            P("fsdp"),
            P("ctx", "fsdp"),
            P("fsdp"),
        ),
        out_specs=(P("ctx", "fsdp"), P("ctx", "fsdp")),
        check_vma=False,
    )
```
